32 devices in a mesh: ens: 2 (over y), wide: 4 (over z), lev: 2 (over x), fld: 2 (over core).
Axes of the slice: x: 2, y: 2, z: 4, core: 2. Of those that a mesh axis runs over, the one named last changes fastest.
Arguments:
- fourier_input_rows: bfloat16 [4, 1280, 4, 4, 256], P('ens', 'wide', None, 'fld', 'lev'), parts along dimension 0, may hold values from -6 to 6
- legendre: bfloat16 [4, 1280, 1280], P('wide', ('lev', 'fld')), may hold values from -0.15625 to 0.15625
- slot_wave: int32 [4], P('wide'), may hold values from 0 to 1279, as said below
- to_modes: bfloat16 [128, 128], replicated, may hold values from -0.5 to 0.5
- from_modes: bfloat16 [128, 128], replicated, may hold values from -0.5 to 0.5
- mode_rate: float32 [128], replicated, may hold values from 0.05 to 5
Outputs:
- fourier_out: bfloat16 [4, 1280, 4, 4, 256], P('ens', 'wide', None, 'fld', 'lev'), parts along dimension 0
- spectral: bfloat16 [8, 1280, 4, 256], P(('ens', 'wide'), None, 'fld', 'lev'), parts along dimension 0
The draws below stay inside these ranges and needn't reach their ends.
There are 2 independent parts, one for each index of `ens`. The reference program is written for one: setup_inputs(seed, part) draws one part's arguments, and reference() takes and returns one part's arrays. A program takes and returns all parts, laid end to end along the dimension named above; an argument that names none is the same for every part. Nothing has to cross between parts.
Inputs may be any that keep to these rules, and one draw needn't show every extreme that they name: `slot_wave`: the wavenumbers of the slots are distinct; one slot holds 0 and one holds 1279.
All inputs are finite; a program needn't handle non-finite values.
Results may differ from the reference program's by a relative error of at most 0.0065.
Values may be sent and summed in bfloat16 or wider, within the bound.
A program may use at most 64 MiB of HBM per device.

```python
import math
import jax
import jax.numpy as jnp
from jax import lax

DEGREE_LIMIT = 1280
HALF_LATITUDES = 1280
FIELD_TOTAL = 4
SLOT_TOTAL = 4
LEVEL_TOTAL = 128


def draw_slot_wave(key, part):
    first_key, second_random_key = jax.random.split(key)
    inner_loop_body = (jax.random.permutation(first_key, DEGREE_LIMIT - 2) + 1).astype(jnp.int32)
    selected_option = jnp.concatenate((jnp.array([0, DEGREE_LIMIT - 1], dtype=jnp.int32), inner_loop_body[:SLOT_TOTAL - 2]))
    ordering_index = jax.random.permutation(second_random_key, SLOT_TOTAL)
    return selected_option[ordering_index].astype(jnp.int32)


def steps_of(stream_key, shape, cuts, smallest, largest):
    factor_of, own = 1.0, jax.random.fold_in(stream_key, 6)
    for dim, parts in cuts:
        draws = jnp.exp(jax.random.uniform(jax.random.fold_in(own, dim), (parts,), jnp.float32, smallest / len(cuts), largest / len(cuts)))
        factor_of = factor_of * jnp.repeat(draws, shape[dim] // parts).reshape([-1 if axis == dim else 1 for axis in range(len(shape))])
    return factor_of


def scatter_about(key, extent, width, limit, cuts=(), kind=jnp.bfloat16):
    level = steps_of(key, extent, cuts, -0.22, 0.18) if cuts else 1.0
    drawn = jax.random.normal(key, extent, jnp.float32) * width * level
    return jnp.minimum(jnp.maximum(drawn, -limit), limit).astype(kind)


def setup_inputs(seed: int = 0, part: int = 0) -> dict:
    splits = jax.random.split(jax.random.key(seed), 7)
    part_splits = jax.random.split(jax.random.fold_in(splits[6], part), 7)
    return {
        "fourier_input_rows": scatter_about(part_splits[0], (2, HALF_LATITUDES, SLOT_TOTAL, FIELD_TOTAL, 2 * LEVEL_TOTAL), 1.0, 6.0, ((1, 4), (3, 2), (4, 2))),
        "legendre": scatter_about(splits[1], (SLOT_TOTAL, DEGREE_LIMIT, HALF_LATITUDES), HALF_LATITUDES ** -0.5, 0.15625, ((0, 4), (1, 4))),
        "slot_wave": draw_slot_wave(jax.random.fold_in(splits[6], 71), part),
        "to_modes": scatter_about(splits[3], (LEVEL_TOTAL, LEVEL_TOTAL), LEVEL_TOTAL ** -0.5, 0.5),
        "from_modes": scatter_about(splits[4], (LEVEL_TOTAL, LEVEL_TOTAL), LEVEL_TOTAL ** -0.5, 0.5),
        "mode_rate": jnp.clip(jnp.exp(jax.random.uniform(splits[5], (LEVEL_TOTAL,), jnp.float32, math.log(0.05), math.log(5.0))), 0.05, 5.0),
    }


def latitude_weights(count):
    position = jnp.arange(count, dtype=jnp.float32)
    return jnp.sin(math.pi * (position + 0.5) / (2 * count))


def reference(fourier_input_rows, legendre, slot_wave, to_modes, from_modes, mode_rate):
    weights = latitude_weights(HALF_LATITUDES)[:, None, None, None]
    north_half = fourier_input_rows[0].astype(jnp.float32)
    south_half = fourier_input_rows[1].astype(jnp.float32)
    symmetric = (weights * (north_half + south_half)).astype(jnp.bfloat16)
    antisym = (weights * (north_half - south_half)).astype(jnp.bfloat16)
    paired = jnp.moveaxis(jnp.concatenate((symmetric, antisym), axis=3), 1, 0)
    column_count = 2 * LEVEL_TOTAL
    degree = jnp.arange(DEGREE_LIMIT, dtype=jnp.int32)
    degree_real = degree.astype(jnp.float32)
    factor = 1.0 + degree_real[:, None] * (degree_real[:, None] + 1.0) * mode_rate[None, :] / (DEGREE_LIMIT * DEGREE_LIMIT)
    weight_in = to_modes.astype(jnp.float32)
    weight_out = from_modes.astype(jnp.float32)

    def one_slot(slot_items):
        table, block_data, slot_number = slot_items
        product = jnp.dot(table, block_data.reshape(HALF_LATITUDES, FIELD_TOTAL * 2 * column_count), preferred_element_type=jnp.float32)
        product = product.reshape(DEGREE_LIMIT, FIELD_TOTAL, 2 * column_count)
        relative = degree - slot_number
        is_live = (relative >= 0)[:, None, None]
        is_even = (relative % 2 == 0)[:, None, None]
        picked = jnp.where(is_even, product[..., :column_count], product[..., column_count:])
        raw_spectral = jnp.where(is_live, picked, jnp.zeros_like(picked)).astype(jnp.bfloat16)
        level_grid = raw_spectral.astype(jnp.float32).reshape(DEGREE_LIMIT, FIELD_TOTAL, LEVEL_TOTAL, 2)
        projected = jnp.einsum("kl,nflr->nfkr", weight_in, level_grid)
        mode_values = (projected / factor[:, None, :, None]).astype(jnp.bfloat16)
        spectral_slot = jnp.einsum("lk,nfkr->nflr", weight_out, mode_values.astype(jnp.float32))
        spectral_slot = spectral_slot.astype(jnp.bfloat16).reshape(DEGREE_LIMIT, FIELD_TOTAL, column_count)
        even_mask = ((relative >= 0) & (relative % 2 == 0))[:, None, None]
        odd_mask = ((relative >= 0) & (relative % 2 == 1))[:, None, None]
        empty_rows = jnp.zeros_like(spectral_slot)
        parity_split = jnp.concatenate((jnp.where(even_mask, spectral_slot, empty_rows), jnp.where(odd_mask, spectral_slot, empty_rows)), axis=2)
        running = jnp.dot(table.T, parity_split.reshape(DEGREE_LIMIT, FIELD_TOTAL * 2 * column_count), preferred_element_type=jnp.float32)
        running = running.reshape(HALF_LATITUDES, FIELD_TOTAL, 2 * column_count)
        even_sum = running[..., :column_count]
        odd_sum = running[..., column_count:]
        fourier_slot = jnp.stack((even_sum + odd_sum, even_sum - odd_sum), axis=0).astype(jnp.bfloat16)
        return fourier_slot, spectral_slot

    fourier_slots, spectral = lax.map(one_slot, (legendre, paired, slot_wave))
    fourier_out = jnp.moveaxis(fourier_slots, 0, 2)
    return fourier_out, spectral
```

```python
import functools
import math

import jax
import jax.numpy as jnp
from jax import lax
from jax.experimental import pallas as pl
from jax.experimental.pallas import tpu as pltpu
from jax.sharding import PartitionSpec as P

MESH = pl.DeviceIdType.MESH


def rows_in(total, most):
    size = most
    while total % size:
        size -= 16
    return size


def latitude_weights(first, count, total):
    position = first + jnp.arange(count, dtype=jnp.int32)
    return jnp.sin(math.pi * (position.astype(jnp.float32) + 0.5) / (2 * total))


def expand(matrix_ref, columns):
    levels = matrix_ref.shape[0]
    hot = lax.broadcasted_iota(jnp.int32, (columns, levels), 0) >> 1
    level = lax.broadcasted_iota(jnp.int32, (columns, levels), 1)
    pick = jnp.where(hot == level, 1.0, 0.0).astype(jnp.bfloat16)
    last = (((1,), (1,)), ((), ()))
    tall = lax.dot_general(pick, matrix_ref[...], last, preferred_element_type=jnp.float32)
    wide = lax.dot_general(
        tall.astype(jnp.bfloat16), pick, last, preferred_element_type=jnp.float32
    )
    row = lax.broadcasted_iota(jnp.int32, (columns, columns), 0)
    col = lax.broadcasted_iota(jnp.int32, (columns, columns), 1)
    return jnp.where(((row ^ col) & 1) == 0, wide, 0.0).astype(jnp.bfloat16)


def step(
    sizes, wave_ref, x_ref, leg_ref, to_ref, from_ref, rate_ref,
    out_ref, spec_ref,
    table, turned, waves, raw_out, raw_in, spec_out, parity, sending, into, back,
    in_send, in_recv, leg_send, leg_recv, leg_local, fwd_send, fwd_recv,
    raw_send, raw_recv, spec_send, spec_recv, out_send, out_recv,
):
    wide, lev = sizes
    fields, _, own_rows, pair = x_ref.shape
    columns = pair // 2
    own_degrees, latitudes = leg_ref.shape
    degrees = table.shape[0]
    part = degrees // lev
    me_w = lax.axis_index("wide")
    me_l = lax.axis_index("lev")
    me_f = lax.axis_index("fld")

    barrier = pltpu.get_barrier_semaphore()
    for k in range(1, wide):
        pl.semaphore_signal(
            barrier, 1, device_id={"wide": lax.rem(me_w + k, wide)}, device_id_type=MESH
        )
    for k in range(1, lev):
        pl.semaphore_signal(
            barrier, 1, device_id={"lev": lax.rem(me_l + k, lev)}, device_id_type=MESH
        )
    pl.semaphore_signal(barrier, 1, device_id={"fld": 1 - me_f}, device_id_type=MESH)
    pl.semaphore_wait(barrier, wide + lev - 1)

    def in_copy(f, k):
        there = lax.rem(me_w + k, wide)
        return pltpu.make_async_remote_copy(
            src_ref=x_ref.at[f, there], dst_ref=waves.at[f, me_w],
            send_sem=in_send.at[f, k], recv_sem=in_recv.at[f, k],
            device_id={"wide": there}, device_id_type=MESH,
        )

    def quarter(l, c):
        start = pl.multiple_of((l * 2 + c) * own_degrees, 16)
        return table.at[pl.ds(start, own_degrees)]

    def leg_copy(k):
        there = lax.rem(me_l + k, lev)
        return pltpu.make_async_remote_copy(
            src_ref=leg_ref, dst_ref=quarter(me_l, me_f),
            send_sem=leg_send.at[k], recv_sem=leg_recv.at[k],
            device_id={"lev": there}, device_id_type=MESH,
        )

    def fwd_copy(k):
        owner = lax.rem(me_l - k + lev, lev)
        return pltpu.make_async_remote_copy(
            src_ref=leg_ref if k == 0 else quarter(owner, me_f), dst_ref=quarter(owner, me_f),
            send_sem=fwd_send.at[k], recv_sem=fwd_recv.at[k],
            device_id={"fld": 1 - me_f}, device_id_type=MESH,
        )

    in_copies = [[in_copy(f, k) for k in range(1, wide)] for f in range(fields)]
    leg_copies = [leg_copy(k) for k in range(1, lev)]
    fwd_copies = [fwd_copy(k) for k in range(lev)]
    for copy in in_copies[0]:
        copy.start()
    for copy in leg_copies:
        copy.start()
    fwd_copies[0].start()
    local = [pltpu.make_async_copy(leg_ref, quarter(me_l, me_f), leg_local.at[0])]
    for f in range(fields):
        local.append(
            pltpu.make_async_copy(x_ref.at[f, me_w], waves.at[f, me_w], leg_local.at[1 + f])
        )
    for copy in local:
        copy.start()

    whole_into = expand(to_ref, lev * columns)
    whole_back = expand(from_ref, lev * columns)
    for l in range(lev):
        into[l] = whole_into[l * columns : (l + 1) * columns, :]
        back[l] = whole_back[:, l * columns : (l + 1) * columns]

    for k in range(1, lev):
        leg_copies[k - 1].wait_recv()
        fwd_copies[k].start()
    for copy in in_copies[0]:
        copy.wait_send()
    for f in range(1, fields):
        for copy in in_copies[f]:
            copy.start()
    for copy in local:
        copy.wait()
    for copy in fwd_copies:
        copy.wait_recv()

    @pl.loop(0, degrees // 128)
    def _(i):
        start = pl.multiple_of(i * 128, 128)
        turned[:, pl.ds(start, 128)] = table[pl.ds(start, 128), :].T

    wave = wave_ref[0]
    direct_rows = rows_in(part, 320)
    for f in range(fields):
        for copy in in_copies[f]:
            copy.wait_recv()

        def raw_copy(k):
            there = lax.rem(me_l + k, lev)
            return pltpu.make_async_remote_copy(
                src_ref=raw_out.at[f, k], dst_ref=raw_in.at[f, k],
                send_sem=raw_send.at[f, k], recv_sem=raw_recv.at[f, k],
                device_id={"lev": there}, device_id_type=MESH,
            )

        raw_copies = [raw_copy(k) for k in range(1, lev)]
        for k in [*range(1, lev), 0]:
            there = lax.rem(me_l + k, lev)

            @pl.loop(0, part // direct_rows)
            def _(i):
                first = pl.multiple_of(there * part + i * direct_rows, 16)
                grid = waves[f].reshape(latitudes, pair).astype(jnp.bfloat16)
                product = jnp.dot(
                    table[pl.ds(first, direct_rows), :], grid, preferred_element_type=jnp.float32
                )
                degree = first + lax.broadcasted_iota(jnp.int32, (direct_rows, columns), 0)
                relative = degree - wave
                picked = jnp.where(
                    (relative & 1) == 0, product[:, :columns], product[:, columns:]
                )
                kept = jnp.where(relative >= 0, picked, 0.0)
                here = pl.multiple_of(i * direct_rows, 16)
                raw_out[f, k, pl.ds(here, direct_rows), :] = kept.astype(jnp.bfloat16)

            if k > 0:
                raw_copies[k - 1].start()
        for copy in raw_copies:
            copy.wait_recv()

        def spec_copy(k):
            there = lax.rem(me_l + k, lev)
            return pltpu.make_async_remote_copy(
                src_ref=spec_out.at[f, k],
                dst_ref=spec_ref.at[f, pl.ds(pl.multiple_of(me_l * part, 16), part)],
                send_sem=spec_send.at[f, k], recv_sem=spec_recv.at[f, k],
                device_id={"lev": there}, device_id_type=MESH,
            )

        @pl.loop(0, part // direct_rows)
        def _(i):
            here = pl.multiple_of(i * direct_rows, 16)
            total = jnp.dot(
                raw_out[f, 0, pl.ds(here, direct_rows), :], into[me_l],
                preferred_element_type=jnp.float32,
            )
            for k in range(1, lev):
                total += jnp.dot(
                    raw_in[f, k, pl.ds(here, direct_rows), :], into[lax.rem(me_l - k + lev, lev)],
                    preferred_element_type=jnp.float32,
                )
            first = me_l * part + here
            degree = first + lax.broadcasted_iota(jnp.int32, total.shape, 0)
            degree = degree.astype(jnp.float32)
            factor = 1.0 + degree * (degree + 1.0) * rate_ref[...] / (degrees * degrees)
            modes = (total / factor).astype(jnp.bfloat16)
            for k in range(lev):
                solved = jnp.dot(
                    modes, back[lax.rem(me_l + k, lev)], preferred_element_type=jnp.float32
                ).astype(jnp.bfloat16)
                if k == 0:
                    spec_ref[f, pl.ds(pl.multiple_of(first, 16), direct_rows), :] = solved
                else:
                    spec_out[f, k, pl.ds(here, direct_rows), :] = solved

        spec_copies = [spec_copy(k) for k in range(1, lev)]
        for copy in spec_copies:
            copy.start()
        for copy in spec_copies:
            copy.wait_recv()

        @pl.loop(0, degrees // direct_rows)
        def _(i):
            first = pl.multiple_of(i * direct_rows, 16)
            values = spec_ref[f, pl.ds(first, direct_rows), :]
            degree = first + lax.broadcasted_iota(jnp.int32, (direct_rows, columns), 0)
            relative = degree - wave
            live = jnp.where(relative >= 0, values.astype(jnp.float32), 0.0)
            is_even = (relative & 1) == 0
            parity[pl.ds(first, direct_rows), :columns] = jnp.where(is_even, live, 0.0).astype(
                jnp.bfloat16
            )
            parity[pl.ds(first, direct_rows), columns:] = jnp.where(is_even, 0.0, live).astype(
                jnp.bfloat16
            )

        def out_copy(k):
            there = lax.rem(me_w + k, wide)
            return pltpu.make_async_remote_copy(
                src_ref=sending.at[f, k], dst_ref=out_ref.at[f, me_w],
                send_sem=out_send.at[f, k], recv_sem=out_recv.at[f, k],
                device_id={"wide": there}, device_id_type=MESH,
            )

        out_copies = [out_copy(k) for k in range(1, wide)]
        for k in [*range(1, wide), 0]:
            there = lax.rem(me_w + k, wide)
            first = pl.multiple_of(there * own_rows, 8)
            sums = jnp.dot(
                turned[pl.ds(first, own_rows), :], parity[...], preferred_element_type=jnp.float32
            )
            north = (sums[:, :columns] + sums[:, columns:]).astype(sending.dtype)
            south = (sums[:, :columns] - sums[:, columns:]).astype(sending.dtype)
            if k == 0:
                out_ref[f, me_w, :, :columns] = north
                out_ref[f, me_w, :, columns:] = south
            else:
                sending[f, k, :, :columns] = north
                sending[f, k, :, columns:] = south
                out_copies[k - 1].start()
        if f == 0:
            later = []
        later.append((raw_copies, spec_copies, out_copies))

    for copy in leg_copies + fwd_copies:
        copy.wait_send()
    for f in range(1, fields):
        for copy in in_copies[f]:
            copy.wait_send()
    for raw_copies, spec_copies, out_copies in later:
        for copy in raw_copies + spec_copies:
            copy.wait_send()
        for copy in out_copies:
            copy.wait_send()
            copy.wait_recv()


def shards(fourier_input_rows, legendre, slot_wave, to_modes, from_modes, mode_rate):
    _, own_rows, slots, fields, columns = fourier_input_rows.shape
    wide = lax.axis_size("wide")
    lev = lax.axis_size("lev")
    own_degrees, latitudes = legendre.shape[1:]
    degrees = own_degrees * lev * 2
    part = degrees // lev
    held = jnp.bfloat16 if own_rows % 16 == 0 else jnp.float32
    weights = latitude_weights(lax.axis_index("wide") * own_rows, own_rows, latitudes)
    weights = weights[:, None, None, None]
    north_half = fourier_input_rows[0].astype(jnp.float32)
    south_half = fourier_input_rows[1].astype(jnp.float32)
    symmetric = (weights * (north_half + south_half)).astype(jnp.bfloat16)
    antisym = (weights * (north_half - south_half)).astype(jnp.bfloat16)
    paired = jnp.concatenate((symmetric, antisym), axis=3)
    paired = jnp.transpose(paired, (2, 1, 0, 3)).astype(held)
    rates = jnp.repeat(mode_rate, 2)[None, :]
    vmem = pl.BlockSpec(memory_space=pltpu.VMEM)
    smem = pl.BlockSpec(memory_space=pltpu.SMEM)
    dma = pltpu.SemaphoreType.DMA
    out, spec = pl.pallas_call(
        functools.partial(step, (wide, lev)),
        out_shape=(
            jax.ShapeDtypeStruct((fields, wide, own_rows, 2 * columns), held),
            jax.ShapeDtypeStruct((fields, degrees, columns), jnp.bfloat16),
        ),
        in_specs=[smem, vmem, vmem, vmem, vmem, vmem],
        out_specs=(vmem, vmem),
        scratch_shapes=[
            pltpu.VMEM((degrees, latitudes), jnp.bfloat16),
            pltpu.VMEM((latitudes, degrees), jnp.bfloat16),
            pltpu.VMEM((fields, wide, own_rows, 2 * columns), held),
            pltpu.VMEM((fields, lev, part, columns), jnp.bfloat16),
            pltpu.VMEM((fields, lev, part, columns), jnp.bfloat16),
            pltpu.VMEM((fields, lev, part, columns), jnp.bfloat16),
            pltpu.VMEM((degrees, 2 * columns), jnp.bfloat16),
            pltpu.VMEM((fields, wide, own_rows, 2 * columns), held),
            pltpu.VMEM((lev, columns, lev * columns), jnp.bfloat16),
            pltpu.VMEM((lev, lev * columns, columns), jnp.bfloat16),
            dma((fields, wide)),
            dma((fields, wide)),
            dma((lev,)),
            dma((lev,)),
            dma((1 + fields,)),
            dma((lev,)),
            dma((lev,)),
            dma((fields, lev)),
            dma((fields, lev)),
            dma((fields, lev)),
            dma((fields, lev)),
            dma((fields, wide)),
            dma((fields, wide)),
        ],
        compiler_params=pltpu.CompilerParams(
            collective_id=0, has_side_effects=True, vmem_limit_bytes=56 * 2**20
        ),
    )(slot_wave, paired, legendre[0], to_modes, from_modes, rates)
    halves = out.astype(jnp.bfloat16).reshape(fields, wide, own_rows, 2, columns)
    fourier_out = jnp.transpose(halves, (3, 2, 1, 0, 4))
    spectral = jnp.transpose(spec, (1, 0, 2))[None]
    return (fourier_out, spectral)


def solution(mesh):
    in_specs = (
        P("ens", "wide", None, "fld", "lev"),
        P("wide", ("lev", "fld"), None),
        P("wide"),
        P(),
        P(),
        P(),
    )
    out_specs = (P("ens", "wide", None, "fld", "lev"), P(("ens", "wide"), None, "fld", "lev"))
    return jax.shard_map(shards, mesh=mesh, in_specs=in_specs, out_specs=out_specs, check_vma=False)
```

```python
import functools
import math

import jax
import jax.numpy as jnp
import numpy as np
from jax import lax
from jax.experimental import pallas as pl
from jax.experimental.pallas import tpu as pltpu
from jax.sharding import PartitionSpec as P

MESH = pl.DeviceIdType.MESH


def rows_in(total, most):
    size = most
    while total % size:
        size -= 16
    return size


def latitude_weights(total, columns):
    position = np.arange(total, dtype=np.float64)
    weights = np.sin(math.pi * (position + 0.5) / (2 * total)).astype(np.float32)
    return jnp.asarray(np.ascontiguousarray(np.broadcast_to(weights[:, None], (total, columns))))


def expand_rates(rate_ref, columns):
    levels = rate_ref.shape[1]
    hot = lax.broadcasted_iota(jnp.int32, (columns, levels), 0) >> 1
    level = lax.broadcasted_iota(jnp.int32, (columns, levels), 1)
    pick = jnp.where(hot == level, 1.0, 0.0)
    return lax.dot_general(
        jnp.broadcast_to(rate_ref[...], (8, levels)), pick, (((1,), (1,)), ((), ())),
        precision=lax.Precision.HIGHEST, preferred_element_type=jnp.float32,
    )


def expand(matrix_ref, columns):
    levels = matrix_ref.shape[0]
    hot = lax.broadcasted_iota(jnp.int32, (columns, levels), 0) >> 1
    level = lax.broadcasted_iota(jnp.int32, (columns, levels), 1)
    pick = jnp.where(hot == level, 1.0, 0.0).astype(jnp.bfloat16)
    last = (((1,), (1,)), ((), ()))
    tall = lax.dot_general(pick, matrix_ref[...], last, preferred_element_type=jnp.float32)
    wide = lax.dot_general(
        tall.astype(jnp.bfloat16), pick, last, preferred_element_type=jnp.float32
    )
    row = lax.broadcasted_iota(jnp.int32, (columns, columns), 0)
    col = lax.broadcasted_iota(jnp.int32, (columns, columns), 1)
    return jnp.where(((row ^ col) & 1) == 0, wide, 0.0).astype(jnp.bfloat16)


def step(
    sizes, wave_ref, given_ref, weight_ref, leg_ref, to_ref, from_ref, rate_ref,
    fourier_ref, spectral_ref,
    weights, single, x_ref, table, turned, waves, raw_out, raw_in, spec_out, spec_ref, parity,
    sending, out_ref, spec_single, into, back, rates,
    in_send, in_recv, leg_send, leg_recv, local_sem, ens_send, ens_recv, own_send, own_recv,
    fwd_send, fwd_recv, raw_send, raw_recv, spec_send, spec_recv, out_send, out_recv,
):
    ens, wide, lev, chunks = sizes
    fields, _, _, own_rows, columns = x_ref.shape
    own_degrees, latitudes = leg_ref.shape
    degrees = table.shape[0]
    part = degrees // lev
    per_row = wide * fields
    me_e = lax.axis_index("ens")
    me_w = lax.axis_index("wide")
    me_l = lax.axis_index("lev")
    me_f = lax.axis_index("fld")

    barrier = pltpu.get_barrier_semaphore()
    for axis, size, me in (("wide", wide, me_w), ("lev", lev, me_l), ("ens", ens, me_e)):
        for k in range(1, size):
            pl.semaphore_signal(
                barrier, 1, device_id={axis: lax.rem(me + k, size)}, device_id_type=MESH
            )
    pl.semaphore_signal(barrier, 1, device_id={"fld": 1 - me_f}, device_id_type=MESH)

    def quarter(l, c):
        start = pl.multiple_of((l * 2 + c) * own_degrees, 16)
        return table.at[pl.ds(start, own_degrees)]

    weight_rows = pl.multiple_of(me_w * own_rows, 8)
    weight_copy = pltpu.make_async_copy(
        weight_ref.at[pl.ds(weight_rows, own_rows)], weights, local_sem.at[0]
    )
    weight_copy.start()
    table_copy = pltpu.make_async_copy(leg_ref, quarter(me_l, me_f), local_sem.at[1])
    table_copy.start()

    total_rows = own_rows * per_row
    piece = total_rows // 5

    for h in range(2):

        @pl.loop(0, 5)
        def _(i):
            rows = pl.ds(pl.multiple_of(i * piece, 16), piece)
            single[h, rows, :] = given_ref[h, rows, :].astype(jnp.float32)

    weight_copy.wait()
    pl.semaphore_wait(barrier, ens + wide + lev - 2)

    def in_copy(f, k):
        there = lax.rem(me_w + k, wide)
        return pltpu.make_async_remote_copy(
            src_ref=x_ref.at[f, there], dst_ref=waves.at[f, me_w],
            send_sem=in_send.at[f, k], recv_sem=in_recv.at[f, k],
            device_id={"wide": there}, device_id_type=MESH,
        )

    share = own_degrees // (ens * chunks)

    def rows_of(l, c, e, i):
        start = (l * 2 + c) * own_degrees + (e * chunks + i) * share
        return table.at[pl.ds(pl.multiple_of(start, 16), share)]

    def leg_copy(k, i):
        start = pl.multiple_of((me_e * chunks + i) * share, 16)
        return pltpu.make_async_remote_copy(
            src_ref=leg_ref.at[pl.ds(start, share)], dst_ref=rows_of(me_l, me_f, me_e, i),
            send_sem=leg_send.at[k, i], recv_sem=leg_recv.at[k, i],
            device_id={"lev": lax.rem(me_l + k, lev)}, device_id_type=MESH,
        )

    def ens_copy(k, q, i):
        rows = rows_of(lax.rem(me_l - k + lev, lev), me_f, me_e, i)
        return pltpu.make_async_remote_copy(
            src_ref=rows, dst_ref=rows,
            send_sem=ens_send.at[k, q, i], recv_sem=ens_recv.at[k, q, i],
            device_id={"ens": lax.rem(me_e + q, ens)}, device_id_type=MESH,
        )

    def fwd_copy(k, q, i):
        rows = rows_of(
            lax.rem(me_l - k + lev, lev), me_f, lax.rem(me_e - q + ens, ens), i
        )
        return pltpu.make_async_remote_copy(
            src_ref=rows, dst_ref=rows,
            send_sem=fwd_send.at[k, q, i], recv_sem=fwd_recv.at[k, q, i],
            device_id={"fld": 1 - me_f}, device_id_type=MESH,
        )

    own_copy = pltpu.make_async_remote_copy(
        src_ref=leg_ref, dst_ref=quarter(me_l, me_f),
        send_sem=own_send.at[0], recv_sem=own_recv.at[0],
        device_id={"fld": 1 - me_f}, device_id_type=MESH,
    )

    def pair_rows(f, s, ref, slot):
        rows = pl.ds(s * fields + f, own_rows, stride=per_row)
        north = single[0, rows, :]
        south = single[1, rows, :]
        plus = (weights[...] * (north + south)).astype(jnp.bfloat16)
        minus = (weights[...] * (north - south)).astype(jnp.bfloat16)
        ref[f, slot, 0] = plus.astype(ref.dtype)
        ref[f, slot, 1] = minus.astype(ref.dtype)

    order = sorted(range(1, wide), key=lambda k: -min(k, wide - k))
    in_copies = [[in_copy(f, k) for k in order] for f in range(fields)]
    leg_copies = [[leg_copy(k, i) for i in range(chunks)] for k in range(1, lev)]
    ens_copies = [
        [[ens_copy(k, q, i) for i in range(chunks)] for q in range(1, ens)] for k in range(1, lev)
    ]
    fwd_copies = [
        [[fwd_copy(k, q, i) for i in range(chunks)] for q in range(ens)] for k in range(1, lev)
    ]
    for row in leg_copies:
        for copy in row:
            copy.start()
    for k, copy in zip(order, in_copies[0]):
        there = lax.rem(me_w + k, wide)
        pair_rows(0, there, x_ref, there)
        copy.start()
    own_copy.start()
    for f in range(fields):
        pair_rows(f, me_w, waves, me_w)
    for f in range(1, fields):
        for k in order:
            there = lax.rem(me_w + k, wide)
            pair_rows(f, there, x_ref, there)

    rates[...] = expand_rates(rate_ref, lev * columns)
    whole_into = expand(to_ref, lev * columns)
    whole_back = expand(from_ref, lev * columns)
    for l in range(lev):
        into[l] = whole_into[l * columns : (l + 1) * columns, :]
        back[l] = whole_back[:, l * columns : (l + 1) * columns]

    for i in range(chunks + 1):
        for k in range(lev - 1):
            if i < chunks:
                leg_copies[k][i].wait_recv()
                for q in range(ens - 1):
                    ens_copies[k][q][i].start()
                fwd_copies[k][0][i].start()
            if i > 0:
                for q in range(ens - 1):
                    ens_copies[k][q][i - 1].wait_recv()
                    fwd_copies[k][q + 1][i - 1].start()
    for copy in in_copies[0]:
        copy.wait_send()
    for f in range(1, fields):
        for copy in in_copies[f]:
            copy.start()
    table_copy.wait()
    own_copy.wait_recv()
    for k in range(lev - 1):
        for q in range(ens):
            for i in range(chunks):
                fwd_copies[k][q][i].wait_recv()

    def turn():
        @pl.loop(0, degrees // 128)
        def _(i):
            start = pl.multiple_of(i * 128, 128)
            turned[:, pl.ds(start, 128)] = table[pl.ds(start, 128), :].T

    wave = wave_ref[0]
    direct_rows = rows_in(part, 320)
    for f in range(fields):
        for copy in in_copies[f]:
            copy.wait_recv()

        def raw_copy(k):
            there = lax.rem(me_l + k, lev)
            return pltpu.make_async_remote_copy(
                src_ref=raw_out.at[f, k], dst_ref=raw_in.at[f, k],
                send_sem=raw_send.at[f, k], recv_sem=raw_recv.at[f, k],
                device_id={"lev": there}, device_id_type=MESH,
            )

        raw_copies = [raw_copy(k) for k in range(1, lev)]
        for k in [*range(1, lev), 0]:
            there = lax.rem(me_l + k, lev)

            @pl.loop(0, part // direct_rows)
            def _(i):
                first = pl.multiple_of(there * part + i * direct_rows, 16)
                grid = jnp.concatenate(
                    [waves[f, :, h].reshape(latitudes, columns) for h in range(2)], axis=1
                ).astype(jnp.bfloat16)
                product = jnp.dot(
                    table[pl.ds(first, direct_rows), :], grid, preferred_element_type=jnp.float32
                )
                degree = first + lax.broadcasted_iota(jnp.int32, (direct_rows, columns), 0)
                relative = degree - wave
                picked = jnp.where(
                    (relative & 1) == 0, product[:, :columns], product[:, columns:]
                )
                kept = jnp.where(relative >= 0, picked, 0.0)
                here = pl.multiple_of(i * direct_rows, 16)
                raw_out[f, k, pl.ds(here, direct_rows), :] = kept.astype(jnp.bfloat16)

            if k > 0:
                raw_copies[k - 1].start()
        if f == 0:
            turn()
        for copy in raw_copies:
            copy.wait_recv()

        def spec_copy(k):
            there = lax.rem(me_l + k, lev)
            return pltpu.make_async_remote_copy(
                src_ref=spec_out.at[f, k],
                dst_ref=spec_ref.at[f, pl.ds(pl.multiple_of(me_l * part, 16), part)],
                send_sem=spec_send.at[f, k], recv_sem=spec_recv.at[f, k],
                device_id={"lev": there}, device_id_type=MESH,
            )

        @pl.loop(0, part // direct_rows)
        def _(i):
            here = pl.multiple_of(i * direct_rows, 16)
            total = jnp.dot(
                raw_out[f, 0, pl.ds(here, direct_rows), :], into[me_l],
                preferred_element_type=jnp.float32,
            )
            for k in range(1, lev):
                total += jnp.dot(
                    raw_in[f, k, pl.ds(here, direct_rows), :], into[lax.rem(me_l - k + lev, lev)],
                    preferred_element_type=jnp.float32,
                )
            first = me_l * part + here
            degree = first + lax.broadcasted_iota(jnp.int32, total.shape, 0)
            degree = degree.astype(jnp.float32)
            factor = 1.0 + degree * (degree + 1.0) * rates[0:1, :] / (degrees * degrees)
            modes = (total / factor).astype(jnp.bfloat16)
            for k in range(lev):
                solved = jnp.dot(
                    modes, back[lax.rem(me_l + k, lev)], preferred_element_type=jnp.float32
                ).astype(jnp.bfloat16)
                if k == 0:
                    spec_ref[f, pl.ds(pl.multiple_of(first, 16), direct_rows), :] = solved
                else:
                    spec_out[f, k, pl.ds(here, direct_rows), :] = solved

        spec_copies = [spec_copy(k) for k in range(1, lev)]
        for copy in spec_copies:
            copy.start()
        for copy in spec_copies:
            copy.wait_recv()

        @pl.loop(0, degrees // direct_rows)
        def _(i):
            first = pl.multiple_of(i * direct_rows, 16)
            values = spec_ref[f, pl.ds(first, direct_rows), :]
            degree = first + lax.broadcasted_iota(jnp.int32, (direct_rows, columns), 0)
            relative = degree - wave
            values = values.astype(jnp.float32)
            spec_single[pl.ds(first * fields + f, direct_rows, stride=fields), :] = values
            live = jnp.where(relative >= 0, values, 0.0)
            is_even = (relative & 1) == 0
            parity[pl.ds(first, direct_rows), :columns] = jnp.where(is_even, live, 0.0).astype(
                jnp.bfloat16
            )
            parity[pl.ds(first, direct_rows), columns:] = jnp.where(is_even, 0.0, live).astype(
                jnp.bfloat16
            )

        def out_copy(k):
            there = lax.rem(me_w + k, wide)
            return pltpu.make_async_remote_copy(
                src_ref=sending.at[f, k], dst_ref=out_ref.at[f, me_w],
                send_sem=out_send.at[f, k], recv_sem=out_recv.at[f, k],
                device_id={"wide": there}, device_id_type=MESH,
            )

        out_copies = [out_copy(k) for k in order]
        for place, k in enumerate([*order, 0]):
            there = lax.rem(me_w + k, wide)
            first = pl.multiple_of(there * own_rows, 8)
            sums = jnp.dot(
                turned[pl.ds(first, own_rows), :], parity[...], preferred_element_type=jnp.float32
            )
            north = (sums[:, :columns] + sums[:, columns:]).astype(sending.dtype)
            south = (sums[:, :columns] - sums[:, columns:]).astype(sending.dtype)
            if k == 0:
                out_ref[f, me_w, 0] = north
                out_ref[f, me_w, 1] = south
            else:
                sending[f, k, 0] = north
                sending[f, k, 1] = south
                out_copies[place].start()
        if f == 0:
            later = []
        later.append((raw_copies, spec_copies, out_copies))

    @pl.loop(0, degrees // direct_rows)
    def _(i):
        count = direct_rows * fields
        rows = pl.ds(pl.multiple_of(i * count, 16), count)
        spectral_ref[rows, :] = spec_single[rows, :].astype(jnp.bfloat16)

    own_copy.wait_send()
    for k in range(lev - 1):
        for i in range(chunks):
            leg_copies[k][i].wait_send()
            for q in range(ens):
                fwd_copies[k][q][i].wait_send()
            for q in range(ens - 1):
                ens_copies[k][q][i].wait_send()
    for f in range(1, fields):
        for copy in in_copies[f]:
            copy.wait_send()
    for raw_copies, spec_copies, _ in later:
        for copy in raw_copies + spec_copies:
            copy.wait_send()

    def place_rows(f, s):
        for h in range(2):
            rows = pl.ds(s * fields + f, own_rows, stride=per_row)
            single[h, rows, :] = out_ref[f, s, h].astype(jnp.float32)

    for f in range(fields):
        place_rows(f, me_w)
    for f in range(fields):
        for k, copy in zip(order, later[f][2]):
            copy.wait_recv()
            place_rows(f, lax.rem(me_w - k + wide, wide))
    for h in range(2):

        @pl.loop(0, 5)
        def _(i):
            rows = pl.ds(pl.multiple_of(i * piece, 16), piece)
            fourier_ref[h, rows, :] = single[h, rows, :].astype(jnp.bfloat16)

    for f in range(fields):
        for copy in later[f][2]:
            copy.wait_send()


def shards(fourier_input_rows, legendre, slot_wave, to_modes, from_modes, mode_rate):
    _, own_rows, slots, fields, columns = fourier_input_rows.shape
    ens = lax.axis_size("ens")
    wide = lax.axis_size("wide")
    lev = lax.axis_size("lev")
    own_degrees, latitudes = legendre.shape[1:]
    degrees = own_degrees * lev * 2
    part = degrees // lev
    chunks = 5
    held = jnp.bfloat16 if own_rows % 16 == 0 else jnp.float32
    rows = own_rows * slots * fields
    given = fourier_input_rows.reshape(2, rows, columns)
    vmem = pl.BlockSpec(memory_space=pltpu.VMEM)
    smem = pl.BlockSpec(memory_space=pltpu.SMEM)
    dma = pltpu.SemaphoreType.DMA
    blocks = (fields, wide, 2, own_rows, columns)
    swaps = (fields, lev, part, columns)
    out, spec = pl.pallas_call(
        functools.partial(step, (ens, wide, lev, chunks)),
        out_shape=(
            jax.ShapeDtypeStruct((2, rows, columns), jnp.bfloat16),
            jax.ShapeDtypeStruct((degrees * fields, columns), jnp.bfloat16),
        ),
        in_specs=[smem, vmem, pl.BlockSpec(memory_space=pl.ANY), vmem, vmem, vmem, vmem],
        out_specs=(vmem, vmem),
        scratch_shapes=[
            pltpu.VMEM((own_rows, columns), jnp.float32),
            pltpu.VMEM((2, rows, columns), jnp.float32),
            pltpu.VMEM(blocks, held),
            pltpu.VMEM((degrees, latitudes), jnp.bfloat16),
            pltpu.VMEM((latitudes, degrees), jnp.bfloat16),
            pltpu.VMEM(blocks, held),
            pltpu.VMEM(swaps, jnp.bfloat16),
            pltpu.VMEM(swaps, jnp.bfloat16),
            pltpu.VMEM(swaps, jnp.bfloat16),
            pltpu.VMEM((fields, degrees, columns), jnp.bfloat16),
            pltpu.VMEM((degrees, 2 * columns), jnp.bfloat16),
            pltpu.VMEM(blocks, held),
            pltpu.VMEM(blocks, held),
            pltpu.VMEM((degrees * fields, columns), jnp.float32),
            pltpu.VMEM((lev, columns, lev * columns), jnp.bfloat16),
            pltpu.VMEM((lev, lev * columns, columns), jnp.bfloat16),
            pltpu.VMEM((8, lev * columns), jnp.float32),
            dma((fields, wide)),
            dma((fields, wide)),
            dma((lev, chunks)),
            dma((lev, chunks)),
            dma((2,)),
            dma((lev, ens, chunks)),
            dma((lev, ens, chunks)),
            dma((1,)),
            dma((1,)),
            dma((lev, ens, chunks)),
            dma((lev, ens, chunks)),
            dma((fields, lev)),
            dma((fields, lev)),
            dma((fields, lev)),
            dma((fields, lev)),
            dma((fields, wide)),
            dma((fields, wide)),
        ],
        compiler_params=pltpu.CompilerParams(
            collective_id=0, has_side_effects=True, vmem_limit_bytes=56 * 2**20
        ),
    )(
        slot_wave, given, latitude_weights(latitudes, columns), legendre[0],
        to_modes, from_modes, mode_rate[None, :],
    )
    fourier_out = out.reshape(2, own_rows, slots, fields, columns)
    spectral = spec.reshape(1, degrees, fields, columns)
    return (fourier_out, spectral)


def solution(mesh):
    in_specs = (
        P("ens", "wide", None, "fld", "lev"),
        P("wide", ("lev", "fld"), None),
        P("wide"),
        P(),
        P(),
        P(),
    )
    out_specs = (P("ens", "wide", None, "fld", "lev"), P(("ens", "wide"), None, "fld", "lev"))
    return jax.shard_map(shards, mesh=mesh, in_specs=in_specs, out_specs=out_specs, check_vma=False)
```

```python
import functools
import math

import jax
import jax.numpy as jnp
import numpy as np
from jax import lax
from jax.experimental import pallas as pl
from jax.experimental.pallas import tpu as pltpu
from jax.sharding import PartitionSpec as P

MESH = pl.DeviceIdType.MESH


def rows_in(total, most):
    size = most
    while total % size:
        size -= 16
    return size


def latitude_weights(total, columns):
    position = np.arange(total, dtype=np.float64)
    weights = np.sin(math.pi * (position + 0.5) / (2 * total)).astype(np.float32)
    return jnp.asarray(np.ascontiguousarray(np.broadcast_to(weights[:, None], (total, columns))))


def expand_rates(rate_ref, columns):
    levels = rate_ref.shape[1]
    hot = lax.broadcasted_iota(jnp.int32, (columns, levels), 0) >> 1
    level = lax.broadcasted_iota(jnp.int32, (columns, levels), 1)
    pick = jnp.where(hot == level, 1.0, 0.0)
    return lax.dot_general(
        jnp.broadcast_to(rate_ref[...], (8, levels)), pick, (((1,), (1,)), ((), ())),
        precision=lax.Precision.HIGHEST, preferred_element_type=jnp.float32,
    )


def expand(matrix_ref, columns):
    levels = matrix_ref.shape[0]
    hot = lax.broadcasted_iota(jnp.int32, (columns, levels), 0) >> 1
    level = lax.broadcasted_iota(jnp.int32, (columns, levels), 1)
    pick = jnp.where(hot == level, 1.0, 0.0).astype(jnp.bfloat16)
    last = (((1,), (1,)), ((), ()))
    tall = lax.dot_general(pick, matrix_ref[...], last, preferred_element_type=jnp.float32)
    wide = lax.dot_general(
        tall.astype(jnp.bfloat16), pick, last, preferred_element_type=jnp.float32
    )
    row = lax.broadcasted_iota(jnp.int32, (columns, columns), 0)
    col = lax.broadcasted_iota(jnp.int32, (columns, columns), 1)
    return jnp.where(((row ^ col) & 1) == 0, wide, 0.0).astype(jnp.bfloat16)


def step(
    sizes, wave_ref, given_far, weight_ref, leg_far, to_far, from_far, rate_far,
    fourier_ref, spectral_ref,
    given_ref, to_ref, from_ref, rate_ref, weights, single, x_ref, table, turned, waves, raw_out, raw_in, spec_out, spec_ref, parity,
    sending, out_ref, spec_single, into, back, rates,
    in_send, in_recv, leg_send, leg_recv, local_sem, ens_send, ens_recv, own_send, own_recv,
    fwd_send, fwd_recv, raw_send, raw_recv, spec_send, spec_recv, out_send, out_recv,
):
    ens, wide, lev, chunks = sizes
    fields, _, _, own_rows, columns = x_ref.shape
    own_degrees, latitudes = leg_far.shape
    degrees = table.shape[0]
    part = degrees // lev
    per_row = wide * fields
    me_e = lax.axis_index("ens")
    me_w = lax.axis_index("wide")
    me_l = lax.axis_index("lev")
    me_f = lax.axis_index("fld")

    barrier = pltpu.get_barrier_semaphore()
    for axis, size, me in (("wide", wide, me_w), ("lev", lev, me_l), ("ens", ens, me_e)):
        for k in range(1, size):
            pl.semaphore_signal(
                barrier, 1, device_id={axis: lax.rem(me + k, size)}, device_id_type=MESH
            )
    pl.semaphore_signal(barrier, 1, device_id={"fld": 1 - me_f}, device_id_type=MESH)

    def quarter(l, c):
        start = pl.multiple_of((l * 2 + c) * own_degrees, 16)
        return table.at[pl.ds(start, own_degrees)]

    weight_rows = pl.multiple_of(me_w * own_rows, 8)
    given_copies = [
        pltpu.make_async_copy(given_far.at[h], given_ref.at[h], local_sem.at[h]) for h in range(2)
    ]
    table_copy = pltpu.make_async_copy(leg_far, quarter(me_l, me_f), local_sem.at[2])
    weight_copy = pltpu.make_async_copy(
        weight_ref.at[pl.ds(weight_rows, own_rows)], weights, local_sem.at[3]
    )
    level_copies = [
        pltpu.make_async_copy(to_far, to_ref, local_sem.at[4]),
        pltpu.make_async_copy(from_far, from_ref, local_sem.at[5]),
        pltpu.make_async_copy(rate_far, rate_ref, local_sem.at[6]),
    ]
    for copy in [*given_copies, weight_copy, table_copy, *level_copies]:
        copy.start()

    total_rows = own_rows * per_row
    piece = total_rows // 5

    for h in range(2):
        given_copies[h].wait()

        @pl.loop(0, 5)
        def _(i):
            rows = pl.ds(pl.multiple_of(i * piece, 16), piece)
            single[h, rows, :] = given_ref[h, rows, :].astype(jnp.float32)

    weight_copy.wait()
    pl.semaphore_wait(barrier, ens + wide + lev - 2)

    def in_copy(f, k):
        there = lax.rem(me_w + k, wide)
        return pltpu.make_async_remote_copy(
            src_ref=x_ref.at[f, there], dst_ref=waves.at[f, me_w],
            send_sem=in_send.at[f, k], recv_sem=in_recv.at[f, k],
            device_id={"wide": there}, device_id_type=MESH,
        )

    share = own_degrees // (ens * chunks)

    def rows_of(l, c, e, i):
        start = (l * 2 + c) * own_degrees + (e * chunks + i) * share
        return table.at[pl.ds(pl.multiple_of(start, 16), share)]

    def leg_copy(k, i):
        rows = rows_of(me_l, me_f, me_e, i)
        return pltpu.make_async_remote_copy(
            src_ref=rows, dst_ref=rows,
            send_sem=leg_send.at[k, i], recv_sem=leg_recv.at[k, i],
            device_id={"lev": lax.rem(me_l + k, lev)}, device_id_type=MESH,
        )

    def ens_copy(k, q, i):
        rows = rows_of(lax.rem(me_l - k + lev, lev), me_f, me_e, i)
        return pltpu.make_async_remote_copy(
            src_ref=rows, dst_ref=rows,
            send_sem=ens_send.at[k, q, i], recv_sem=ens_recv.at[k, q, i],
            device_id={"ens": lax.rem(me_e + q, ens)}, device_id_type=MESH,
        )

    def fwd_copy(k, q, i):
        rows = rows_of(
            lax.rem(me_l - k + lev, lev), me_f, lax.rem(me_e - q + ens, ens), i
        )
        return pltpu.make_async_remote_copy(
            src_ref=rows, dst_ref=rows,
            send_sem=fwd_send.at[k, q, i], recv_sem=fwd_recv.at[k, q, i],
            device_id={"fld": 1 - me_f}, device_id_type=MESH,
        )

    own_copy = pltpu.make_async_remote_copy(
        src_ref=quarter(me_l, me_f), dst_ref=quarter(me_l, me_f),
        send_sem=own_send.at[0], recv_sem=own_recv.at[0],
        device_id={"fld": 1 - me_f}, device_id_type=MESH,
    )

    def pair_rows(f, s, ref, slot):
        rows = pl.ds(s * fields + f, own_rows, stride=per_row)
        north = single[0, rows, :]
        south = single[1, rows, :]
        plus = (weights[...] * (north + south)).astype(jnp.bfloat16)
        minus = (weights[...] * (north - south)).astype(jnp.bfloat16)
        ref[f, slot, 0] = plus.astype(ref.dtype)
        ref[f, slot, 1] = minus.astype(ref.dtype)

    order = sorted(range(1, wide), key=lambda k: -min(k, wide - k))
    in_copies = [[in_copy(f, k) for k in order] for f in range(fields)]
    leg_copies = [[leg_copy(k, i) for i in range(chunks)] for k in range(1, lev)]
    ens_copies = [
        [[ens_copy(k, q, i) for i in range(chunks)] for q in range(1, ens)] for k in range(1, lev)
    ]
    fwd_copies = [
        [[fwd_copy(k, q, i) for i in range(chunks)] for q in range(ens)] for k in range(1, lev)
    ]
    table_copy.wait()
    for row in leg_copies:
        for copy in row:
            copy.start()
    for k, copy in zip(order, in_copies[0]):
        there = lax.rem(me_w + k, wide)
        pair_rows(0, there, x_ref, there)
        copy.start()
    own_copy.start()
    for f in range(fields):
        pair_rows(f, me_w, waves, me_w)
    for f in range(1, fields):
        for k in order:
            there = lax.rem(me_w + k, wide)
            pair_rows(f, there, x_ref, there)

    for copy in level_copies:
        copy.wait()
    rates[...] = expand_rates(rate_ref, lev * columns)
    whole_into = expand(to_ref, lev * columns)
    whole_back = expand(from_ref, lev * columns)
    for l in range(lev):
        into[l] = whole_into[l * columns : (l + 1) * columns, :]
        back[l] = whole_back[:, l * columns : (l + 1) * columns]

    for i in range(chunks + 1):
        for k in range(lev - 1):
            if i < chunks:
                leg_copies[k][i].wait_recv()
                for q in range(ens - 1):
                    ens_copies[k][q][i].start()
                fwd_copies[k][0][i].start()
            if i > 0:
                for q in range(ens - 1):
                    ens_copies[k][q][i - 1].wait_recv()
                    fwd_copies[k][q + 1][i - 1].start()
    for copy in in_copies[0]:
        copy.wait_send()
    for f in range(1, fields):
        for copy in in_copies[f]:
            copy.start()
    own_copy.wait_recv()
    for k in range(lev - 1):
        for q in range(ens):
            for i in range(chunks):
                fwd_copies[k][q][i].wait_recv()

    def turn():
        @pl.loop(0, degrees // 128)
        def _(i):
            start = pl.multiple_of(i * 128, 128)
            turned[:, pl.ds(start, 128)] = table[pl.ds(start, 128), :].T

    wave = wave_ref[0]
    direct_rows = rows_in(part, 320)
    pieces = part // direct_rows
    for f in range(fields):
        for copy in in_copies[f]:
            copy.wait_recv()

        def raw_copy(k, i):
            there = lax.rem(me_l + k, lev)
            rows = pl.ds(i * direct_rows, direct_rows)
            return pltpu.make_async_remote_copy(
                src_ref=raw_out.at[f, k, rows], dst_ref=raw_in.at[f, k, rows],
                send_sem=raw_send.at[f, k, i], recv_sem=raw_recv.at[f, k, i],
                device_id={"lev": there}, device_id_type=MESH,
            )

        raw_copies = [[raw_copy(k, i) for i in range(pieces)] for k in range(1, lev)]
        def direct(k, i):
            first = pl.multiple_of(lax.rem(me_l + k, lev) * part + i * direct_rows, 16)
            grid = jnp.concatenate(
                [waves[f, :, h].reshape(latitudes, columns) for h in range(2)], axis=1
            ).astype(jnp.bfloat16)
            product = jnp.dot(
                table[pl.ds(first, direct_rows), :], grid, preferred_element_type=jnp.float32
            )
            degree = first + lax.broadcasted_iota(jnp.int32, (direct_rows, columns), 0)
            relative = degree - wave
            picked = jnp.where((relative & 1) == 0, product[:, :columns], product[:, columns:])
            kept = jnp.where(relative >= 0, picked, 0.0)
            raw_out[f, k, pl.ds(i * direct_rows, direct_rows), :] = kept.astype(jnp.bfloat16)

        for i in range(pieces):
            for k in range(1, lev):
                direct(k, i)
                raw_copies[k - 1][i].start()
        for i in range(pieces):
            direct(0, i)
        if f == 0:
            turn()

        def spec_copy(k, i):
            there = lax.rem(me_l + k, lev)
            start = pl.multiple_of(me_l * part + i * direct_rows, 16)
            return pltpu.make_async_remote_copy(
                src_ref=spec_out.at[f, k, pl.ds(i * direct_rows, direct_rows)],
                dst_ref=spec_ref.at[f, pl.ds(start, direct_rows)],
                send_sem=spec_send.at[f, k, i], recv_sem=spec_recv.at[f, k, i],
                device_id={"lev": there}, device_id_type=MESH,
            )

        spec_copies = [[spec_copy(k, i) for i in range(pieces)] for k in range(1, lev)]
        for i in range(pieces):
            here = i * direct_rows
            for row in raw_copies:
                row[i].wait_recv()
            total = jnp.dot(
                raw_out[f, 0, pl.ds(here, direct_rows), :], into[me_l],
                preferred_element_type=jnp.float32,
            )
            for k in range(1, lev):
                total += jnp.dot(
                    raw_in[f, k, pl.ds(here, direct_rows), :], into[lax.rem(me_l - k + lev, lev)],
                    preferred_element_type=jnp.float32,
                )
            first = me_l * part + here
            degree = first + lax.broadcasted_iota(jnp.int32, total.shape, 0)
            degree = degree.astype(jnp.float32)
            factor = 1.0 + degree * (degree + 1.0) * rates[0:1, :] / (degrees * degrees)
            modes = (total / factor).astype(jnp.bfloat16)
            for k in range(lev):
                solved = jnp.dot(
                    modes, back[lax.rem(me_l + k, lev)], preferred_element_type=jnp.float32
                ).astype(jnp.bfloat16)
                if k == 0:
                    spec_ref[f, pl.ds(pl.multiple_of(first, 16), direct_rows), :] = solved
                else:
                    spec_out[f, k, pl.ds(here, direct_rows), :] = solved
                    spec_copies[k - 1][i].start()
        for row in spec_copies:
            for copy in row:
                copy.wait_recv()

        @pl.loop(0, degrees // direct_rows)
        def _(i):
            first = pl.multiple_of(i * direct_rows, 16)
            values = spec_ref[f, pl.ds(first, direct_rows), :]
            degree = first + lax.broadcasted_iota(jnp.int32, (direct_rows, columns), 0)
            relative = degree - wave
            values = values.astype(jnp.float32)
            spec_single[pl.ds(first * fields + f, direct_rows, stride=fields), :] = values
            live = jnp.where(relative >= 0, values, 0.0)
            is_even = (relative & 1) == 0
            parity[pl.ds(first, direct_rows), :columns] = jnp.where(is_even, live, 0.0).astype(
                jnp.bfloat16
            )
            parity[pl.ds(first, direct_rows), columns:] = jnp.where(is_even, 0.0, live).astype(
                jnp.bfloat16
            )

        def out_copy(k):
            there = lax.rem(me_w + k, wide)
            return pltpu.make_async_remote_copy(
                src_ref=sending.at[f, k], dst_ref=out_ref.at[f, me_w],
                send_sem=out_send.at[f, k], recv_sem=out_recv.at[f, k],
                device_id={"wide": there}, device_id_type=MESH,
            )

        out_copies = [out_copy(k) for k in order]
        for place, k in enumerate([*order, 0]):
            there = lax.rem(me_w + k, wide)
            first = pl.multiple_of(there * own_rows, 8)
            sums = jnp.dot(
                turned[pl.ds(first, own_rows), :], parity[...], preferred_element_type=jnp.float32
            )
            north = (sums[:, :columns] + sums[:, columns:]).astype(sending.dtype)
            south = (sums[:, :columns] - sums[:, columns:]).astype(sending.dtype)
            if k == 0:
                out_ref[f, me_w, 0] = north
                out_ref[f, me_w, 1] = south
            else:
                sending[f, k, 0] = north
                sending[f, k, 1] = south
                out_copies[place].start()
        if f == 0:
            later = []
        later.append((raw_copies, spec_copies, out_copies))

    @pl.loop(0, degrees // direct_rows)
    def _(i):
        count = direct_rows * fields
        rows = pl.ds(pl.multiple_of(i * count, 16), count)
        spectral_ref[rows, :] = spec_single[rows, :].astype(jnp.bfloat16)

    own_copy.wait_send()
    for k in range(lev - 1):
        for i in range(chunks):
            leg_copies[k][i].wait_send()
            for q in range(ens):
                fwd_copies[k][q][i].wait_send()
            for q in range(ens - 1):
                ens_copies[k][q][i].wait_send()
    for f in range(1, fields):
        for copy in in_copies[f]:
            copy.wait_send()
    for raw_copies, spec_copies, _ in later:
        for row in raw_copies + spec_copies:
            for copy in row:
                copy.wait_send()

    def place_rows(f, s):
        for h in range(2):
            rows = pl.ds(s * fields + f, own_rows, stride=per_row)
            single[h, rows, :] = out_ref[f, s, h].astype(jnp.float32)

    for f in range(fields):
        place_rows(f, me_w)
    for f in range(fields):
        for k, copy in zip(order, later[f][2]):
            copy.wait_recv()
            place_rows(f, lax.rem(me_w - k + wide, wide))
    for h in range(2):

        @pl.loop(0, 5)
        def _(i):
            rows = pl.ds(pl.multiple_of(i * piece, 16), piece)
            fourier_ref[h, rows, :] = single[h, rows, :].astype(jnp.bfloat16)

    for f in range(fields):
        for copy in later[f][2]:
            copy.wait_send()


def shards(fourier_input_rows, legendre, slot_wave, to_modes, from_modes, mode_rate):
    _, own_rows, slots, fields, columns = fourier_input_rows.shape
    ens = lax.axis_size("ens")
    wide = lax.axis_size("wide")
    lev = lax.axis_size("lev")
    own_degrees, latitudes = legendre.shape[1:]
    degrees = own_degrees * lev * 2
    part = degrees // lev
    chunks = 5
    held = jnp.bfloat16 if own_rows % 16 == 0 else jnp.float32
    rows = own_rows * slots * fields
    given = fourier_input_rows.reshape(2, rows, columns)
    vmem = pl.BlockSpec(memory_space=pltpu.VMEM)
    smem = pl.BlockSpec(memory_space=pltpu.SMEM)
    dma = pltpu.SemaphoreType.DMA
    blocks = (fields, wide, 2, own_rows, columns)
    swaps = (fields, lev, part, columns)
    out, spec = pl.pallas_call(
        functools.partial(step, (ens, wide, lev, chunks)),
        out_shape=(
            jax.ShapeDtypeStruct((2, rows, columns), jnp.bfloat16),
            jax.ShapeDtypeStruct((degrees * fields, columns), jnp.bfloat16),
        ),
        in_specs=[smem] + [pl.BlockSpec(memory_space=pltpu.HBM)] * 6,
        out_specs=(vmem, vmem),
        scratch_shapes=[
            pltpu.VMEM((2, rows, columns), jnp.bfloat16),
            pltpu.VMEM(to_modes.shape, jnp.bfloat16),
            pltpu.VMEM(from_modes.shape, jnp.bfloat16),
            pltpu.VMEM((1, mode_rate.shape[0]), jnp.float32),
            pltpu.VMEM((own_rows, columns), jnp.float32),
            pltpu.VMEM((2, rows, columns), jnp.float32),
            pltpu.VMEM(blocks, held),
            pltpu.VMEM((degrees, latitudes), jnp.bfloat16),
            pltpu.VMEM((latitudes, degrees), jnp.bfloat16),
            pltpu.VMEM(blocks, held),
            pltpu.VMEM(swaps, jnp.bfloat16),
            pltpu.VMEM(swaps, jnp.bfloat16),
            pltpu.VMEM(swaps, jnp.bfloat16),
            pltpu.VMEM((fields, degrees, columns), jnp.bfloat16),
            pltpu.VMEM((degrees, 2 * columns), jnp.bfloat16),
            pltpu.VMEM(blocks, held),
            pltpu.VMEM(blocks, held),
            pltpu.VMEM((degrees * fields, columns), jnp.float32),
            pltpu.VMEM((lev, columns, lev * columns), jnp.bfloat16),
            pltpu.VMEM((lev, lev * columns, columns), jnp.bfloat16),
            pltpu.VMEM((8, lev * columns), jnp.float32),
            dma((fields, wide)),
            dma((fields, wide)),
            dma((lev, chunks)),
            dma((lev, chunks)),
            dma((7,)),
            dma((lev, ens, chunks)),
            dma((lev, ens, chunks)),
            dma((1,)),
            dma((1,)),
            dma((lev, ens, chunks)),
            dma((lev, ens, chunks)),
            dma((fields, lev, part // rows_in(part, 320))),
            dma((fields, lev, part // rows_in(part, 320))),
            dma((fields, lev, part // rows_in(part, 320))),
            dma((fields, lev, part // rows_in(part, 320))),
            dma((fields, wide)),
            dma((fields, wide)),
        ],
        compiler_params=pltpu.CompilerParams(
            collective_id=0, has_side_effects=True, vmem_limit_bytes=36 * 2**20
        ),
    )(
        slot_wave, given, latitude_weights(latitudes, columns), legendre[0],
        to_modes, from_modes, mode_rate[None, :],
    )
    fourier_out = out.reshape(2, own_rows, slots, fields, columns)
    spectral = spec.reshape(1, degrees, fields, columns)
    return (fourier_out, spectral)


def solution(mesh):
    in_specs = (
        P("ens", "wide", None, "fld", "lev"),
        P("wide", ("lev", "fld"), None),
        P("wide"),
        P(),
        P(),
        P(),
    )
    out_specs = (P("ens", "wide", None, "fld", "lev"), P(("ens", "wide"), None, "fld", "lev"))
    return jax.shard_map(shards, mesh=mesh, in_specs=in_specs, out_specs=out_specs, check_vma=False)
```

```python
import functools
import math

import jax
import jax.numpy as jnp
import numpy as np
from jax import lax
from jax.experimental import pallas as pl
from jax.experimental.pallas import tpu as pltpu
from jax.sharding import PartitionSpec as P

MESH = pl.DeviceIdType.MESH


def rows_in(total, most):
    size = most
    while total % size:
        size -= 16
    return size


def latitude_weights(total, columns):
    position = np.arange(total, dtype=np.float64)
    weights = np.sin(math.pi * (position + 0.5) / (2 * total)).astype(np.float32)
    return jnp.asarray(np.ascontiguousarray(np.broadcast_to(weights[:, None], (total, columns))))


def expand_rates(rate_ref, columns):
    levels = rate_ref.shape[1]
    hot = lax.broadcasted_iota(jnp.int32, (columns, levels), 0) >> 1
    level = lax.broadcasted_iota(jnp.int32, (columns, levels), 1)
    pick = jnp.where(hot == level, 1.0, 0.0)
    return lax.dot_general(
        jnp.broadcast_to(rate_ref[...], (8, levels)), pick, (((1,), (1,)), ((), ())),
        precision=lax.Precision.HIGHEST, preferred_element_type=jnp.float32,
    )


def expand(matrix_ref, columns):
    levels = matrix_ref.shape[0]
    hot = lax.broadcasted_iota(jnp.int32, (columns, levels), 0) >> 1
    level = lax.broadcasted_iota(jnp.int32, (columns, levels), 1)
    pick = jnp.where(hot == level, 1.0, 0.0).astype(jnp.bfloat16)
    last = (((1,), (1,)), ((), ()))
    tall = lax.dot_general(pick, matrix_ref[...], last, preferred_element_type=jnp.float32)
    wide = lax.dot_general(
        tall.astype(jnp.bfloat16), pick, last, preferred_element_type=jnp.float32
    )
    row = lax.broadcasted_iota(jnp.int32, (columns, columns), 0)
    col = lax.broadcasted_iota(jnp.int32, (columns, columns), 1)
    return jnp.where(((row ^ col) & 1) == 0, wide, 0.0).astype(jnp.bfloat16)


def step(
    sizes, wave_ref, given_ref, weight_ref, leg_ref, to_ref, from_ref, rate_ref,
    fourier_ref, spectral_ref,
    weights, single, x_ref, table, turned, waves, raw_out, raw_in, spec_out, spec_ref, parity,
    sending, out_ref, spec_single, into, back, rates,
    in_send, in_recv, leg_send, leg_recv, local_sem, ens_send, ens_recv, own_send, own_recv,
    fwd_send, fwd_recv, raw_send, raw_recv, spec_send, spec_recv, out_send, out_recv,
):
    ens, wide, lev, chunks = sizes
    fields, _, _, own_rows, columns = x_ref.shape
    own_degrees, latitudes = leg_ref.shape
    degrees = table.shape[0]
    part = degrees // lev
    per_row = wide * fields
    me_e = lax.axis_index("ens")
    me_w = lax.axis_index("wide")
    me_l = lax.axis_index("lev")
    me_f = lax.axis_index("fld")

    barrier = pltpu.get_barrier_semaphore()
    for axis, size, me in (("wide", wide, me_w), ("lev", lev, me_l), ("ens", ens, me_e)):
        for k in range(1, size):
            pl.semaphore_signal(
                barrier, 1, device_id={axis: lax.rem(me + k, size)}, device_id_type=MESH
            )
    pl.semaphore_signal(barrier, 1, device_id={"fld": 1 - me_f}, device_id_type=MESH)

    def quarter(l, c):
        start = pl.multiple_of((l * 2 + c) * own_degrees, 16)
        return table.at[pl.ds(start, own_degrees)]

    weight_rows = pl.multiple_of(me_w * own_rows, 8)
    weight_copy = pltpu.make_async_copy(
        weight_ref.at[pl.ds(weight_rows, own_rows)], weights, local_sem.at[0]
    )
    weight_copy.start()
    table_copy = pltpu.make_async_copy(leg_ref, quarter(me_l, me_f), local_sem.at[1])
    table_copy.start()

    total_rows = own_rows * per_row
    piece = total_rows // 5

    for h in range(2):

        @pl.loop(0, 5)
        def _(i):
            rows = pl.ds(pl.multiple_of(i * piece, 16), piece)
            single[h, rows, :] = given_ref[h, rows, :].astype(jnp.float32)

    weight_copy.wait()
    pl.semaphore_wait(barrier, ens + wide + lev - 2)

    def in_copy(f, k):
        there = lax.rem(me_w + k, wide)
        return pltpu.make_async_remote_copy(
            src_ref=x_ref.at[f, there], dst_ref=waves.at[f, me_w],
            send_sem=in_send.at[f, k], recv_sem=in_recv.at[f, k],
            device_id={"wide": there}, device_id_type=MESH,
        )

    share = own_degrees // (ens * chunks)

    def rows_of(l, c, e, i):
        start = (l * 2 + c) * own_degrees + (e * chunks + i) * share
        return table.at[pl.ds(pl.multiple_of(start, 16), share)]

    def leg_copy(k, i):
        start = pl.multiple_of((me_e * chunks + i) * share, 16)
        return pltpu.make_async_remote_copy(
            src_ref=leg_ref.at[pl.ds(start, share)], dst_ref=rows_of(me_l, me_f, me_e, i),
            send_sem=leg_send.at[k, i], recv_sem=leg_recv.at[k, i],
            device_id={"lev": lax.rem(me_l + k, lev)}, device_id_type=MESH,
        )

    def ens_copy(k, q, i):
        rows = rows_of(lax.rem(me_l - k + lev, lev), me_f, me_e, i)
        return pltpu.make_async_remote_copy(
            src_ref=rows, dst_ref=rows,
            send_sem=ens_send.at[k, q, i], recv_sem=ens_recv.at[k, q, i],
            device_id={"ens": lax.rem(me_e + q, ens)}, device_id_type=MESH,
        )

    def fwd_copy(k, q, i):
        rows = rows_of(
            lax.rem(me_l - k + lev, lev), me_f, lax.rem(me_e - q + ens, ens), i
        )
        return pltpu.make_async_remote_copy(
            src_ref=rows, dst_ref=rows,
            send_sem=fwd_send.at[k, q, i], recv_sem=fwd_recv.at[k, q, i],
            device_id={"fld": 1 - me_f}, device_id_type=MESH,
        )

    own_copy = pltpu.make_async_remote_copy(
        src_ref=leg_ref, dst_ref=quarter(me_l, me_f),
        send_sem=own_send.at[0], recv_sem=own_recv.at[0],
        device_id={"fld": 1 - me_f}, device_id_type=MESH,
    )

    def pair_rows(f, s, ref, slot):
        rows = pl.ds(s * fields + f, own_rows, stride=per_row)
        north = single[0, rows, :]
        south = single[1, rows, :]
        plus = (weights[...] * (north + south)).astype(jnp.bfloat16)
        minus = (weights[...] * (north - south)).astype(jnp.bfloat16)
        ref[f, slot, 0] = plus.astype(ref.dtype)
        ref[f, slot, 1] = minus.astype(ref.dtype)

    order = sorted(range(1, wide), key=lambda k: -min(k, wide - k))
    in_copies = [[in_copy(f, k) for k in order] for f in range(fields)]
    leg_copies = [[leg_copy(k, i) for i in range(chunks)] for k in range(1, lev)]
    ens_copies = [
        [[ens_copy(k, q, i) for i in range(chunks)] for q in range(1, ens)] for k in range(1, lev)
    ]
    fwd_copies = [
        [[fwd_copy(k, q, i) for i in range(chunks)] for q in range(ens)] for k in range(1, lev)
    ]
    for row in leg_copies:
        for copy in row:
            copy.start()
    for k, copy in zip(order, in_copies[0]):
        there = lax.rem(me_w + k, wide)
        pair_rows(0, there, x_ref, there)
        copy.start()
    own_copy.start()
    for f in range(fields):
        pair_rows(f, me_w, waves, me_w)
    for f in range(1, fields):
        for k in order:
            there = lax.rem(me_w + k, wide)
            pair_rows(f, there, x_ref, there)

    rates[...] = expand_rates(rate_ref, lev * columns)
    whole_into = expand(to_ref, lev * columns)
    whole_back = expand(from_ref, lev * columns)
    for l in range(lev):
        into[l] = whole_into[l * columns : (l + 1) * columns, :]
        back[l] = whole_back[:, l * columns : (l + 1) * columns]

    for i in range(chunks + 1):
        for k in range(lev - 1):
            if i < chunks:
                leg_copies[k][i].wait_recv()
                for q in range(ens - 1):
                    ens_copies[k][q][i].start()
                fwd_copies[k][0][i].start()
            if i > 0:
                for q in range(ens - 1):
                    ens_copies[k][q][i - 1].wait_recv()
                    fwd_copies[k][q + 1][i - 1].start()
    for copy in in_copies[0]:
        copy.wait_send()
    for f in range(1, fields):
        for copy in in_copies[f]:
            copy.start()
    table_copy.wait()
    own_copy.wait_recv()
    for k in range(lev - 1):
        for q in range(ens):
            for i in range(chunks):
                fwd_copies[k][q][i].wait_recv()

    def turn():
        @pl.loop(0, degrees // 128)
        def _(i):
            start = pl.multiple_of(i * 128, 128)
            turned[:, pl.ds(start, 128)] = table[pl.ds(start, 128), :].T

    wave = wave_ref[0]
    direct_rows = rows_in(part, 320)
    pieces = part // direct_rows
    for f in range(fields):
        for copy in in_copies[f]:
            copy.wait_recv()

        def raw_copy(k, i):
            there = lax.rem(me_l + k, lev)
            rows = pl.ds(i * direct_rows, direct_rows)
            return pltpu.make_async_remote_copy(
                src_ref=raw_out.at[f, k, rows], dst_ref=raw_in.at[f, k, rows],
                send_sem=raw_send.at[f, k, i], recv_sem=raw_recv.at[f, k, i],
                device_id={"lev": there}, device_id_type=MESH,
            )

        raw_copies = [[raw_copy(k, i) for i in range(pieces)] for k in range(1, lev)]
        def direct(k, i):
            first = pl.multiple_of(lax.rem(me_l + k, lev) * part + i * direct_rows, 16)
            grid = jnp.concatenate(
                [waves[f, :, h].reshape(latitudes, columns) for h in range(2)], axis=1
            ).astype(jnp.bfloat16)
            product = jnp.dot(
                table[pl.ds(first, direct_rows), :], grid, preferred_element_type=jnp.float32
            )
            degree = first + lax.broadcasted_iota(jnp.int32, (direct_rows, columns), 0)
            relative = degree - wave
            picked = jnp.where((relative & 1) == 0, product[:, :columns], product[:, columns:])
            kept = jnp.where(relative >= 0, picked, 0.0)
            raw_out[f, k, pl.ds(i * direct_rows, direct_rows), :] = kept.astype(jnp.bfloat16)

        for i in range(pieces):
            for k in range(1, lev):
                direct(k, i)
                raw_copies[k - 1][i].start()
        for i in range(pieces):
            direct(0, i)
        if f == 0:
            turn()

        def spec_copy(k, i):
            there = lax.rem(me_l + k, lev)
            start = pl.multiple_of(me_l * part + i * direct_rows, 16)
            return pltpu.make_async_remote_copy(
                src_ref=spec_out.at[f, k, pl.ds(i * direct_rows, direct_rows)],
                dst_ref=spec_ref.at[f, pl.ds(start, direct_rows)],
                send_sem=spec_send.at[f, k, i], recv_sem=spec_recv.at[f, k, i],
                device_id={"lev": there}, device_id_type=MESH,
            )

        spec_copies = [[spec_copy(k, i) for i in range(pieces)] for k in range(1, lev)]
        for i in range(pieces):
            here = i * direct_rows
            for row in raw_copies:
                row[i].wait_recv()
            total = jnp.dot(
                raw_out[f, 0, pl.ds(here, direct_rows), :], into[me_l],
                preferred_element_type=jnp.float32,
            )
            for k in range(1, lev):
                total += jnp.dot(
                    raw_in[f, k, pl.ds(here, direct_rows), :], into[lax.rem(me_l - k + lev, lev)],
                    preferred_element_type=jnp.float32,
                )
            first = me_l * part + here
            degree = first + lax.broadcasted_iota(jnp.int32, total.shape, 0)
            degree = degree.astype(jnp.float32)
            factor = 1.0 + degree * (degree + 1.0) * rates[0:1, :] / (degrees * degrees)
            modes = (total / factor).astype(jnp.bfloat16)
            for k in range(lev):
                solved = jnp.dot(
                    modes, back[lax.rem(me_l + k, lev)], preferred_element_type=jnp.float32
                ).astype(jnp.bfloat16)
                if k == 0:
                    spec_ref[f, pl.ds(pl.multiple_of(first, 16), direct_rows), :] = solved
                else:
                    spec_out[f, k, pl.ds(here, direct_rows), :] = solved
                    spec_copies[k - 1][i].start()
        for row in spec_copies:
            for copy in row:
                copy.wait_recv()

        @pl.loop(0, degrees // direct_rows)
        def _(i):
            first = pl.multiple_of(i * direct_rows, 16)
            values = spec_ref[f, pl.ds(first, direct_rows), :]
            degree = first + lax.broadcasted_iota(jnp.int32, (direct_rows, columns), 0)
            relative = degree - wave
            values = values.astype(jnp.float32)
            spec_single[pl.ds(first * fields + f, direct_rows, stride=fields), :] = values
            live = jnp.where(relative >= 0, values, 0.0)
            is_even = (relative & 1) == 0
            parity[pl.ds(first, direct_rows), :columns] = jnp.where(is_even, live, 0.0).astype(
                jnp.bfloat16
            )
            parity[pl.ds(first, direct_rows), columns:] = jnp.where(is_even, 0.0, live).astype(
                jnp.bfloat16
            )

        def out_copy(k):
            there = lax.rem(me_w + k, wide)
            return pltpu.make_async_remote_copy(
                src_ref=sending.at[f, k], dst_ref=out_ref.at[f, me_w],
                send_sem=out_send.at[f, k], recv_sem=out_recv.at[f, k],
                device_id={"wide": there}, device_id_type=MESH,
            )

        out_copies = [out_copy(k) for k in order]
        for place, k in enumerate([*order, 0]):
            there = lax.rem(me_w + k, wide)
            first = pl.multiple_of(there * own_rows, 8)
            sums = jnp.dot(
                turned[pl.ds(first, own_rows), :], parity[...], preferred_element_type=jnp.float32
            )
            north = (sums[:, :columns] + sums[:, columns:]).astype(sending.dtype)
            south = (sums[:, :columns] - sums[:, columns:]).astype(sending.dtype)
            if k == 0:
                out_ref[f, me_w, 0] = north
                out_ref[f, me_w, 1] = south
            else:
                sending[f, k, 0] = north
                sending[f, k, 1] = south
                out_copies[place].start()
        if f == 0:
            later = []
        later.append((raw_copies, spec_copies, out_copies))

    @pl.loop(0, degrees // direct_rows)
    def _(i):
        count = direct_rows * fields
        rows = pl.ds(pl.multiple_of(i * count, 16), count)
        spectral_ref[rows, :] = spec_single[rows, :].astype(jnp.bfloat16)

    own_copy.wait_send()
    for k in range(lev - 1):
        for i in range(chunks):
            leg_copies[k][i].wait_send()
            for q in range(ens):
                fwd_copies[k][q][i].wait_send()
            for q in range(ens - 1):
                ens_copies[k][q][i].wait_send()
    for f in range(1, fields):
        for copy in in_copies[f]:
            copy.wait_send()
    for raw_copies, spec_copies, _ in later:
        for row in raw_copies + spec_copies:
            for copy in row:
                copy.wait_send()

    def place_rows(f, s):
        for h in range(2):
            rows = pl.ds(s * fields + f, own_rows, stride=per_row)
            single[h, rows, :] = out_ref[f, s, h].astype(jnp.float32)

    for f in range(fields):
        place_rows(f, me_w)
    for f in range(fields):
        for k, copy in zip(order, later[f][2]):
            copy.wait_recv()
            place_rows(f, lax.rem(me_w - k + wide, wide))
    for h in range(2):

        @pl.loop(0, 5)
        def _(i):
            rows = pl.ds(pl.multiple_of(i * piece, 16), piece)
            fourier_ref[h, rows, :] = single[h, rows, :].astype(jnp.bfloat16)

    for f in range(fields):
        for copy in later[f][2]:
            copy.wait_send()


def shards(fourier_input_rows, legendre, slot_wave, to_modes, from_modes, mode_rate):
    _, own_rows, slots, fields, columns = fourier_input_rows.shape
    ens = lax.axis_size("ens")
    wide = lax.axis_size("wide")
    lev = lax.axis_size("lev")
    own_degrees, latitudes = legendre.shape[1:]
    degrees = own_degrees * lev * 2
    part = degrees // lev
    chunks = 5
    held = jnp.bfloat16 if own_rows % 16 == 0 else jnp.float32
    rows = own_rows * slots * fields
    given = fourier_input_rows.reshape(2, rows, columns)
    vmem = pl.BlockSpec(memory_space=pltpu.VMEM)
    smem = pl.BlockSpec(memory_space=pltpu.SMEM)
    dma = pltpu.SemaphoreType.DMA
    blocks = (fields, wide, 2, own_rows, columns)
    swaps = (fields, lev, part, columns)
    out, spec = pl.pallas_call(
        functools.partial(step, (ens, wide, lev, chunks)),
        out_shape=(
            jax.ShapeDtypeStruct((2, rows, columns), jnp.bfloat16),
            jax.ShapeDtypeStruct((degrees * fields, columns), jnp.bfloat16),
        ),
        in_specs=[smem, vmem, pl.BlockSpec(memory_space=pl.ANY), vmem, vmem, vmem, vmem],
        out_specs=(vmem, vmem),
        scratch_shapes=[
            pltpu.VMEM((own_rows, columns), jnp.float32),
            pltpu.VMEM((2, rows, columns), jnp.float32),
            pltpu.VMEM(blocks, held),
            pltpu.VMEM((degrees, latitudes), jnp.bfloat16),
            pltpu.VMEM((latitudes, degrees), jnp.bfloat16),
            pltpu.VMEM(blocks, held),
            pltpu.VMEM(swaps, jnp.bfloat16),
            pltpu.VMEM(swaps, jnp.bfloat16),
            pltpu.VMEM(swaps, jnp.bfloat16),
            pltpu.VMEM((fields, degrees, columns), jnp.bfloat16),
            pltpu.VMEM((degrees, 2 * columns), jnp.bfloat16),
            pltpu.VMEM(blocks, held),
            pltpu.VMEM(blocks, held),
            pltpu.VMEM((degrees * fields, columns), jnp.float32),
            pltpu.VMEM((lev, columns, lev * columns), jnp.bfloat16),
            pltpu.VMEM((lev, lev * columns, columns), jnp.bfloat16),
            pltpu.VMEM((8, lev * columns), jnp.float32),
            dma((fields, wide)),
            dma((fields, wide)),
            dma((lev, chunks)),
            dma((lev, chunks)),
            dma((2,)),
            dma((lev, ens, chunks)),
            dma((lev, ens, chunks)),
            dma((1,)),
            dma((1,)),
            dma((lev, ens, chunks)),
            dma((lev, ens, chunks)),
            dma((fields, lev, part // rows_in(part, 320))),
            dma((fields, lev, part // rows_in(part, 320))),
            dma((fields, lev, part // rows_in(part, 320))),
            dma((fields, lev, part // rows_in(part, 320))),
            dma((fields, wide)),
            dma((fields, wide)),
        ],
        compiler_params=pltpu.CompilerParams(
            collective_id=0, has_side_effects=True, vmem_limit_bytes=56 * 2**20
        ),
    )(
        slot_wave, given, latitude_weights(latitudes, columns), legendre[0],
        to_modes, from_modes, mode_rate[None, :],
    )
    fourier_out = out.reshape(2, own_rows, slots, fields, columns)
    spectral = spec.reshape(1, degrees, fields, columns)
    return (fourier_out, spectral)


def solution(mesh):
    in_specs = (
        P("ens", "wide", None, "fld", "lev"),
        P("wide", ("lev", "fld"), None),
        P("wide"),
        P(),
        P(),
        P(),
    )
    out_specs = (P("ens", "wide", None, "fld", "lev"), P(("ens", "wide"), None, "fld", "lev"))
    return jax.shard_map(shards, mesh=mesh, in_specs=in_specs, out_specs=out_specs, check_vma=False)
```
